256 devices in a mesh: tile: 32 (over z_lo, y, core), head: 8 (over x, z_hi).
Axes of the slice: x: 4, y: 4, z: 8 (z_hi: 2, z_lo: 4; z = z_hi * 4 + z_lo), core: 2. Of those that a mesh axis runs over, the one named last changes fastest.
Arguments:
- queries: bfloat16 [8192, 5120], P('tile', 'head'), may hold values from -5 to 5
- keys: bfloat16 [8192, 5120], P('tile', 'head'), may hold values from -12 to 12
- values: bfloat16 [8192, 5120], P('tile', 'head'), may hold values from -6 to 6
- reward_grad: bfloat16 [8192, 5120], P('tile', 'head'), may hold values from -6 to 6
- window_mask: int32 [32, 27], replicated, may hold values from 0 to 1, as said below
Outputs:
- attended: bfloat16 [8192, 5120], P('tile', 'head')
- grad_queries: bfloat16 [8192, 5120], P('tile', 'head')
- grad_keys: bfloat16 [8192, 5120], P('tile', 'head')
- grad_values: bfloat16 [8192, 5120], P('tile', 'head')
The draws below stay inside these ranges and needn't reach their ends.
Inputs may be any that keep to these rules, and one draw needn't show every extreme that they name: `window_mask`: entry (a, 13), the tile itself, is always 1; offsets that leave the grid are always 0.
All inputs are finite; a program needn't handle non-finite values.
Results may differ from the reference program's by a relative error of at most 0.01.
Values may be sent and summed in bfloat16 or wider, within the bound.
A program may use at most 128 MiB of HBM per device.

```python
import math
import jax
import jax.numpy as jnp
from jax import lax

HEADS = 40
HD = 128
GH = 4
GW = 2
GT = 4
NTILES = 32
TOK_TILE = 256
TOKENS = 8192
FEAT = 5120


def draw_queries(key, part):
    shape = (TOKENS, HEADS * HD)
    base = jnp.clip(jax.random.normal(jax.random.fold_in(key, 1), shape, jnp.float32), -4.0, 4.0)
    return base.astype(jnp.bfloat16)


def draw_keys(key, part):
    shape = (TOKENS, HEADS * HD)
    spread = jnp.exp(jax.random.uniform(jax.random.fold_in(key, 3), (TOKENS, 1), jnp.float32, 0.0, math.log(4.0)))
    base = jnp.clip(jax.random.normal(jax.random.fold_in(key, 2), shape, jnp.float32), -3.0, 3.0) * spread
    return base.astype(jnp.bfloat16)


def draw_window_mask(key, part):
    tiles = jnp.arange(NTILES, dtype=jnp.int32)
    frame = tiles // (GH * GW)
    row = tiles // GW % GH
    column = tiles % GW
    offsets = jnp.arange(27, dtype=jnp.int32)
    step_t = offsets // 9 - 1
    step_h = offsets // 3 % 3 - 1
    step_w = offsets % 3 - 1
    near_t = frame[:, None] + step_t[None, :]
    near_h = row[:, None] + step_h[None, :]
    near_w = column[:, None] + step_w[None, :]
    inside = (near_t >= 0) & (near_t < GT) & (near_h >= 0) & (near_h < GH) & (near_w >= 0) & (near_w < GW)
    keep = jax.random.randint(key, (NTILES, 27), 0, 4) > 0
    centre = (offsets == 13)[None, :]
    return jnp.where(centre | inside & keep, 1, 0).astype(jnp.int32)


def levels(rng, dims, cuts, smallest, largest):
    gain, own = 1.0, jax.random.fold_in(rng, 6)
    for position, blocks in cuts:
        heights = jnp.exp(jax.random.uniform(jax.random.fold_in(own, position), (blocks,), jnp.float32, smallest / len(cuts), largest / len(cuts)))
        gain = gain * jnp.repeat(heights, dims[position] // blocks).reshape([-1 if axis == position else 1 for axis in range(len(dims))])
    return gain


def gaussian(stream_key, extent, scale, limit, cuts=(), kind=jnp.bfloat16):
    values = scale * jax.random.normal(stream_key, extent, jnp.float32)
    if cuts:
        values = values * levels(stream_key, extent, cuts, -0.22, 0.18)
    return jnp.clip(values, -limit, limit).astype(kind)


def setup_inputs(seed: int = 0) -> dict:
    arg_keys = jax.random.split(jax.random.key(seed), 6)
    return {
        "queries": draw_queries(jax.random.fold_in(arg_keys[5], 71), 0),
        "keys": draw_keys(jax.random.fold_in(arg_keys[5], 71), 0),
        "values": gaussian(arg_keys[2], (TOKENS, FEAT), 1.0, 6.0, ((0, 32), (1, 8))),
        "reward_grad": gaussian(arg_keys[3], (TOKENS, FEAT), 1.0, 6.0, ((0, 32), (1, 8))),
        "window_mask": draw_window_mask(jax.random.fold_in(arg_keys[5], 71), 0),
    }


def slot_tables(window_mask):
    tiles = jnp.arange(NTILES, dtype=jnp.int32)
    frame = tiles // (GH * GW)
    row = tiles // GW % GH
    column = tiles % GW
    slots = jnp.arange(18, dtype=jnp.int32)
    step_t = slots // 6 - 1
    step_h = slots // 2 % 3 - 1
    across = slots % 2
    near_t = frame[:, None] + step_t[None, :]
    near_h = row[:, None] + step_h[None, :]
    inside = (near_t >= 0) & (near_t < GT) & (near_h >= 0) & (near_h < GH)
    sources = jnp.clip(near_t * (GH * GW) + near_h * GW + across[None, :], 0, NTILES - 1).astype(jnp.int32)
    offset = ((step_t + 1) * 9 + (step_h + 1) * 3 + across)[None, :] - column[:, None] + 1
    chosen = jnp.take_along_axis(window_mask, offset.astype(jnp.int32), axis=1)
    return (sources, inside & (chosen == 1))

def reference(queries, keys, values, reward_grad, window_mask):
    sources, valid = slot_tables(window_mask)
    scale = 1.0 / math.sqrt(HD)

    def split(array):
        return jnp.transpose(array.reshape(NTILES, TOK_TILE, HEADS, HD), (2, 0, 1, 3))

    def one_head(pieces):
        query, key_here, value_here, grad_here = pieces
        query32 = query.astype(jnp.float32)
        grad32 = grad_here.astype(jnp.float32)
        near_keys = key_here[sources].astype(jnp.float32)
        near_values = value_here[sources].astype(jnp.float32)
        scores = jnp.einsum('atd,asbd->atsb', query32, near_keys) * scale
        masked = jnp.where(valid[:, None, :, None], scores, -jnp.inf)
        top = lax.optimization_barrier(jnp.max(masked, axis=(2, 3), keepdims=True))
        logsum = top + jnp.log(lax.optimization_barrier(jnp.sum(jnp.exp(masked - top), axis=(2, 3), keepdims=True)))
        weights = jnp.exp(masked - logsum)
        probs = weights.astype(jnp.bfloat16)
        probs32 = probs.astype(jnp.float32)
        output = jnp.einsum('atsb,asbd->atd', probs32, near_values).astype(jnp.bfloat16)
        delta = lax.optimization_barrier(jnp.sum(grad32 * output.astype(jnp.float32), axis=2))[:, :, None, None]
        dprob = jnp.einsum('atd,asbd->atsb', grad32, near_values)
        dscore = (weights * (dprob - delta) * scale).astype(jnp.bfloat16).astype(jnp.float32)
        grad_query = jnp.einsum('atsb,asbd->atd', dscore, near_keys)
        key_parts = jnp.einsum('atsb,atd->asbd', dscore, query32)
        value_parts = jnp.einsum('atsb,atd->asbd', probs32, grad32)
        flat = sources.reshape(-1)
        grad_key = jnp.zeros((NTILES, TOK_TILE, HD), jnp.float32).at[flat].add(key_parts.reshape(-1, TOK_TILE, HD))
        grad_value = jnp.zeros((NTILES, TOK_TILE, HD), jnp.float32).at[flat].add(value_parts.reshape(-1, TOK_TILE, HD))
        return (output, grad_query.astype(jnp.bfloat16), grad_key.astype(jnp.bfloat16), grad_value.astype(jnp.bfloat16))
    results = lax.map(one_head, (split(queries), split(keys), split(values), split(reward_grad)))

    def merge(array):
        return jnp.transpose(array, (1, 2, 0, 3)).reshape(TOKENS, FEAT)
    return (merge(results[0]), merge(results[1]), merge(results[2]), merge(results[3]))
```

```python
import functools
import math

import jax
import jax.numpy as jnp
from jax import lax
from jax.experimental import pallas as pl
from jax.experimental.pallas import tpu as pltpu
from jax.sharding import PartitionSpec as P

HD = 128
GH = 4
GW = 2


QD_LO, QD_HI, KV_LO, KV_HI, KVP = 0, 1, 2, 3, 4
ST_LO, ST_HI, FIN_LO, FIN_HI, OQ_LO, OQ_HI, DKV, DZ_LO, DZ_HI = 7, 8, 9, 10, 11, 12, 13, 14, 15
KINDS = 16

NT = (((1,), (1,)), ((), ()))
NEG = -1e30
BIG = 3e30
MESH = pl.DeviceIdType.MESH


def mm(left, right, dims=(((1,), (0,)), ((), ()))):
    return lax.dot_general(left, right, dims, preferred_element_type=jnp.float32)


def kernel(
    heads,
    tok,
    frames,
    mask_ref,
    q_hbm,
    k_hbm,
    v_hbm,
    g_hbm,
    att_ref,
    gq_ref,
    gk_ref,
    gv_ref,
    qd,
    kv,
    kvt,
    scores,
    ef,
    ovk,
    wt,
    st,
    stin,
    fin,
    oq_out,
    oq_in,
    dkv_own,
    dkv_out,
    dkv_in,
    dz_out,
    dz_in,
    load_sem,
    send_sem,
    recv_sem,
):
    me = lax.axis_index("tile")
    per_frame = GH * GW
    frame = me // per_frame
    row = me // GW % GH
    column = me % GW
    partner = me + 1 - 2 * column
    has_ym, has_yp = row > 0, row < GH - 1
    has_zm, has_zp = frame > 0, frame < frames - 1
    ym, yp, zm, zp = me - GW, me + GW, me - per_frame, me + per_frame
    scale = 1.0 / math.sqrt(HD)
    scale2 = scale * math.log2(math.e)
    bf16, f32 = jnp.bfloat16, jnp.float32

    def rows(slot):
        return pl.ds(slot * tok, tok)

    def table(kind, j):
        if kind in (QD_LO, QD_HI):
            low = kind == QD_LO
            return (
                qd.at[j, rows(1), :],
                qd.at[j, rows(0 if low else 2), :],
                yp if low else ym,
                has_yp if low else has_ym,
                has_ym if low else has_yp,
            )
        if kind in (KV_LO, KV_HI):
            low = kind == KV_LO
            return (
                kv.at[j, rows(1), :],
                kv.at[j, rows(0 if low else 2), :],
                zp if low else zm,
                has_zp if low else has_zm,
                has_zm if low else has_zp,
            )
        if kind in (KVP, KVP + 1, KVP + 2):
            d = kind - KVP
            there = (has_zm, None, has_zp)[d]
            return (kv.at[j, rows(d), :], kv.at[j, rows(3 + d), :], partner, there, there)
        if kind == DKV:
            return (dkv_out.at[j], dkv_in.at[j], partner, None, None)
        if kind in (DZ_LO, DZ_HI):
            low = kind == DZ_LO
            return (
                dz_out.at[j, 1 if low else 0],
                dz_in.at[j, 0 if low else 1],
                zp if low else zm,
                has_zp if low else has_zm,
                has_zm if low else has_zp,
            )
        low = kind in (ST_LO, FIN_LO, OQ_LO)
        if kind in (ST_LO, ST_HI):
            source, target = st.at[j, 2 if low else 0], stin.at[j, 0 if low else 1]
        elif kind in (FIN_LO, FIN_HI):
            source, target = fin.at[j, 1], fin.at[j, 0 if low else 2]
        else:
            source, target = oq_out.at[j, 1 if low else 0], oq_in.at[j, 0 if low else 1]
        return (
            source,
            target,
            yp if low else ym,
            has_yp if low else has_ym,
            has_ym if low else has_yp,
        )

    def copy_of(kind, j):
        source, target, device, sent, received = table(kind, j)
        copy = pltpu.make_async_remote_copy(
            src_ref=source,
            dst_ref=target,
            send_sem=send_sem.at[kind, j],
            recv_sem=recv_sem.at[kind, j],
            device_id={"tile": device},
            device_id_type=MESH,
        )
        return copy, sent, received

    def guarded(condition, action):
        if condition is None:
            action()
        else:
            pl.when(condition)(action)

    def send(kind, j):
        copy, sent, _ = copy_of(kind, j)
        guarded(sent, copy.start)

    def arrive(kind, j):
        copy, _, received = copy_of(kind, j)
        guarded(received, copy.wait_recv)

    def sent_off(kind, j):
        copy, sent, _ = copy_of(kind, j)
        guarded(sent, copy.wait_send)

    def start_load(j, _):
        start = pl.multiple_of(j * HD, HD)
        for which, ref, buffer, lane in (
            (0, g_hbm, qd, 0),
            (0, q_hbm, qd, HD),
            (1, v_hbm, kv, 0),
            (1, k_hbm, kv, HD),
        ):
            pltpu.make_async_copy(
                ref.at[:, pl.ds(start, HD)],
                buffer.at[j, rows(1), pl.ds(lane, HD)],
                load_sem.at[which, j],
            ).start()
        return 0

    lax.fori_loop(0, heads, start_load, 0)

    def blank(j, _):
        for missing, slot in ((row == 0, 0), (row == GH - 1, 2)):
            @pl.when(missing)
            def _():
                side = slot // 2
                qd[j, rows(slot), :] = jnp.zeros((tok, 2 * HD), bf16)
                stin[j, side] = jnp.concatenate(
                    [jnp.full((1, tok), NEG, f32), jnp.zeros((7, tok), f32)], axis=0
                )
                fin[j, slot] = jnp.zeros((8, tok), f32)
                oq_in[j, side] = jnp.zeros((2 * HD, tok), bf16)

        for missing, slot in ((frame == 0, 0), (frame == frames - 1, 2)):
            @pl.when(missing)
            def _():
                kv[j, rows(slot), :] = jnp.zeros((tok, 2 * HD), bf16)
                kv[j, rows(3 + slot), :] = jnp.zeros((tok, 2 * HD), bf16)
                dz_in[j, slot // 2] = jnp.zeros((tok, 2 * HD), bf16)

        return 0

    barrier = pltpu.get_barrier_semaphore()

    def greet(device):
        pl.semaphore_signal(barrier, inc=1, device_id={"tile": device}, device_id_type=MESH)

    greet(partner)
    for there, device in ((has_ym, ym), (has_yp, yp), (has_zm, zm), (has_zp, zp)):
        pl.when(there)(functools.partial(greet, device))
    lax.fori_loop(0, heads, blank, 0)
    peers = sum(jnp.where(there, 1, 0) for there in (has_ym, has_yp, has_zm, has_zp))
    pl.semaphore_wait(barrier, 1 + peers)

    def send_own(j, _):
        for which, buffer in ((1, kv), (0, qd)):
            own = buffer.at[j, rows(1), :]
            pltpu.make_async_copy(own, own, load_sem.at[which, j]).wait()
            for kind in ((KV_LO, KV_HI, KVP + 1), (QD_LO, QD_HI))[1 - which]:
                send(kind, j)
        return 0

    lax.fori_loop(0, heads, send_own, 0)

    def relay(j):
        for kind, onward in ((KV_LO, KVP), (KV_HI, KVP + 2)):
            arrive(kind, j)
            send(onward, j)

    relay(0)

    def prepare(j):
        for kind in (KVP, KVP + 1, KVP + 2, QD_LO, QD_HI):
            arrive(kind, j)
        for kt in range(6):
            kvt[:, rows(kt)] = kv[j, rows(kt), :].T

    def forward(j, s):
        ring = lax.rem(j, 2)
        qrows = pl.ds(pl.multiple_of(s * tok, tok), tok)
        tile = me + (s - 1) * GW
        near = row + s - 1
        exists = jnp.where((near >= 0) & (near < GH), 1, 0)
        tile = jnp.where(exists == 1, tile, me)
        drops = []
        for kt in range(6):
            across = 1 if kt < 3 else 2 - 2 * column
            flag = mask_ref[tile, kt % 3 * 9 + (2 - s) * 3 + across] * exists
            drops.append((1 - flag).astype(f32))
        query = qd[j, qrows, HD:]
        grad = qd[j, qrows, :HD]
        top = jnp.full((1, tok), NEG, f32)
        for kt in range(6):
            block = mm(kv[j, rows(kt), HD:], query, NT) * scale2
            scores[rows(kt), :] = block
            top = jnp.maximum(top, jnp.max(block, axis=0, keepdims=True) + drops[kt] * NEG)
        total = jnp.zeros((1, tok), f32)
        moment = jnp.zeros((1, tok), f32)
        ecols = pl.ds(pl.multiple_of(s * 2 * tok, tok), tok)
        fcols = pl.ds(pl.multiple_of((s * 2 + 1) * tok, tok), tok)
        for kt in range(6):
            weight = jnp.exp2(scores[rows(kt), :] - (top + drops[kt] * BIG))
            slope = weight * mm(kv[j, rows(kt), :HD], grad, NT)
            total += jnp.sum(weight, axis=0, keepdims=True)
            moment += jnp.sum(slope, axis=0, keepdims=True)
            ef[ring, rows(kt), ecols] = weight.astype(bf16)
            ef[ring, rows(kt), fcols] = slope.astype(bf16)
        ovk[j, s, : 2 * HD, :] = mm(kvt[...], ef[ring, :, ecols])
        ovk[j, s, 2 * HD :, :] = mm(kvt[HD:, :], ef[ring, :, fcols])
        st[j, s, 0:1, :] = top
        st[j, s, 1:2, :] = total
        st[j, s, 2:3, :] = moment

    def combine(j):
        arrive(ST_LO, j)
        arrive(ST_HI, j)
        parts = (stin.at[j, 0], st.at[j, 1], stin.at[j, 1])
        tops = [part[0:1, :] for part in parts]
        top = jnp.maximum(jnp.maximum(tops[0], tops[1]), tops[2])
        shares = [jnp.exp2(one - top) for one in tops]
        total = sum(share * part[1:2, :] for share, part in zip(shares, parts))
        moment = sum(share * part[2:3, :] for share, part in zip(shares, parts))
        inverse = 1.0 / total
        fin[j, 1, 0:1, :] = top
        fin[j, 1, 1:2, :] = inverse
        fin[j, 1, 2:3, :] = moment * inverse
        send(FIN_LO, j)
        send(FIN_HI, j)

    def backward(j):
        ring = lax.rem(j, 2)
        arrive(FIN_LO, j)
        arrive(FIN_HI, j)
        for s in (0, 2, 1):
            share = jnp.exp2(st[j, s, 0:1, :] - fin[j, s, 0:1, :]) * fin[j, s, 1:2, :]
            delta = fin[j, s, 2:3, :]
            scaled = share * scale
            output = ovk[j, s, :HD, :] * share
            grad_query = (ovk[j, s, 2 * HD :, :] - delta * ovk[j, s, HD : 2 * HD, :]) * scaled
            if s == 1:
                ovk[j, s, :HD, :] = output
                ovk[j, s, HD : 2 * HD, :] = grad_query
            else:
                oq_out[j, s // 2, :HD, :] = output.astype(bf16)
                oq_out[j, s // 2, HD:, :] = grad_query.astype(bf16)
                send(OQ_HI if s == 0 else OQ_LO, j)
            flipped = qd[j, rows(s), :].astype(f32).T
            ecols = pl.ds(s * 2 * tok, tok)
            fcols = pl.ds((s * 2 + 1) * tok, tok)
            wt[:HD, ecols] = (flipped[:HD] * share).astype(bf16)
            wt[HD:, ecols] = (flipped[HD:] * (-scaled * delta)).astype(bf16)
            wt[:HD, fcols] = jnp.zeros((HD, tok), bf16)
            wt[HD:, fcols] = (flipped[HD:] * scaled).astype(bf16)
        for kt in (3, 4, 5, 0, 1, 2):
            part = mm(ef[ring, rows(kt), :], wt[...], NT)
            if kt < 3:
                dkv_own[j, kt] = part
            else:
                dkv_out[j, kt - 3] = part.astype(bf16)
            if kt == 5:
                send(DKV, j)

    def hand_back(j):
        arrive(DKV, j)
        for d, kind in ((0, DZ_HI), (2, DZ_LO)):
            dz_out[j, d // 2] = (dkv_own[j, d] + dkv_in[j, d].astype(f32)).astype(bf16)
            send(kind, j)

    def finish(j):
        for kind in (OQ_LO, OQ_HI, DZ_LO, DZ_HI):
            arrive(kind, j)
        cols = pl.ds(pl.multiple_of(j * HD, HD), HD)
        both = ovk[j, 1, : 2 * HD, :] + oq_in[j, 0].astype(f32) + oq_in[j, 1].astype(f32)
        both = both.T
        att_ref[:, cols] = both[:, :HD].astype(bf16)
        gq_ref[:, cols] = both[:, HD:].astype(bf16)
        both = dkv_own[j, 1] + dkv_in[j, 1].astype(f32)
        both = both + dz_in[j, 0].astype(f32) + dz_in[j, 1].astype(f32)
        gv_ref[:, cols] = both[:, :HD].astype(bf16)
        gk_ref[:, cols] = both[:, HD:].astype(bf16)

    def step(i, _):
        @pl.when(i < heads)
        def _():
            prepare(i)

        def inner(s, _):
            @pl.when(i < heads)
            def _():
                forward(i, s)

                @pl.when(s == 0)
                def _():
                    send(ST_HI, i)

                @pl.when(s == 2)
                def _():
                    send(ST_LO, i)

            @pl.when((s == 0) & (i + 1 < heads))
            def _():
                relay(i + 1)

            @pl.when((s == 0) & (i >= 1) & (i <= heads))
            def _():
                combine(i - 1)

            @pl.when((s == 1) & (i >= 2))
            def _():
                hand_back(i - 2)

            return 0

        lax.fori_loop(0, 3, inner, 0)

        @pl.when((i >= 1) & (i <= heads))
        def _():
            backward(i - 1)

        @pl.when(i >= 2)
        def _():
            finish(i - 2)

        return 0

    lax.fori_loop(0, heads + 2, step, 0)

    def drain(j, _):
        for kind in range(KINDS):
            sent_off(kind, j)
        return 0

    lax.fori_loop(0, heads, drain, 0)


def on_device(queries, keys, values, reward_grad, window_mask):
    tok, width = queries.shape
    heads = width // HD
    frames = lax.axis_size("tile") // (GH * GW)
    bf16, f32 = jnp.bfloat16, jnp.float32
    hbm = pl.BlockSpec(memory_space=pl.ANY)
    vmem = pl.BlockSpec(memory_space=pltpu.VMEM)
    return pl.pallas_call(
        functools.partial(kernel, heads, tok, frames),
        out_shape=[jax.ShapeDtypeStruct((tok, width), bf16)] * 4,
        in_specs=[pl.BlockSpec(memory_space=pltpu.SMEM), hbm, hbm, hbm, hbm],
        out_specs=[vmem] * 4,
        scratch_shapes=[
            pltpu.VMEM((heads, 3 * tok, 2 * HD), bf16),
            pltpu.VMEM((heads, 6 * tok, 2 * HD), bf16),
            pltpu.VMEM((2 * HD, 6 * tok), bf16),
            pltpu.VMEM((6 * tok, tok), f32),
            pltpu.VMEM((2, 6 * tok, 6 * tok), bf16),
            pltpu.VMEM((heads, 3, 3 * HD, tok), f32),
            pltpu.VMEM((2 * HD, 6 * tok), bf16),
            pltpu.VMEM((heads, 3, 8, tok), f32),
            pltpu.VMEM((heads, 2, 8, tok), f32),
            pltpu.VMEM((heads, 3, 8, tok), f32),
            pltpu.VMEM((heads, 2, 2 * HD, tok), bf16),
            pltpu.VMEM((heads, 2, 2 * HD, tok), bf16),
            pltpu.VMEM((heads, 3, tok, 2 * HD), f32),
            pltpu.VMEM((heads, 3, tok, 2 * HD), bf16),
            pltpu.VMEM((heads, 3, tok, 2 * HD), bf16),
            pltpu.VMEM((heads, 2, tok, 2 * HD), bf16),
            pltpu.VMEM((heads, 2, tok, 2 * HD), bf16),
            pltpu.SemaphoreType.DMA((2, heads)),
            pltpu.SemaphoreType.DMA((KINDS, heads)),
            pltpu.SemaphoreType.DMA((KINDS, heads)),
        ],
        compiler_params=pltpu.CompilerParams(
            collective_id=0, has_side_effects=True, vmem_limit_bytes=60 * 1024 * 1024
        ),
    )(window_mask, queries, keys, values, reward_grad)


def solution(mesh):
    return jax.shard_map(
        on_device,
        mesh=mesh,
        in_specs=(P("tile", "head"), P("tile", "head"), P("tile", "head"), P("tile", "head"), P()),
        out_specs=(P("tile", "head"), P("tile", "head"), P("tile", "head"), P("tile", "head")),
        check_vma=False,
    )
```

```python
import functools
import math

import jax
import jax.numpy as jnp
from jax import lax
from jax.experimental import pallas as pl
from jax.experimental.pallas import tpu as pltpu
from jax.sharding import PartitionSpec as P

HD = 128
GH = 4
GW = 2


QD_LO, QD_HI, KV_LO, KV_HI, KVP = 0, 1, 2, 3, 4
ST_LO, ST_HI, FIN_LO, FIN_HI, OQ_LO, OQ_HI, DKV, DZ_LO, DZ_HI = 7, 8, 9, 10, 11, 12, 13, 14, 15
DKV1, DKV2 = 16, 17
KINDS = 18

AHEAD = 2

ONES = 16
ESUM = 2 * HD + ONES

NT = (((1,), (1,)), ((), ()))
NEG = -1e30
BIG = 3e30
MESH = pl.DeviceIdType.MESH


def mm(left, right, dims=(((1,), (0,)), ((), ()))):
    return lax.dot_general(left, right, dims, preferred_element_type=jnp.float32)


def kernel(
    heads,
    tok,
    frames,
    mask_ref,
    q_hbm,
    k_hbm,
    v_hbm,
    g_hbm,
    att_ref,
    gq_ref,
    gk_ref,
    gv_ref,
    qd,
    kv,
    kvt,
    scores,
    slopes,
    limits,
    ef,
    ovk,
    wt,
    st,
    stin,
    fin,
    oq_out,
    oq_in,
    dkv_own,
    dkv_out,
    dkv_in,
    dz_out,
    dz_in,
    result,
    load_sem,
    out_sem,
    send_sem,
    recv_sem,
):
    me = lax.axis_index("tile")
    per_frame = GH * GW
    frame = me // per_frame
    row = me // GW % GH
    column = me % GW
    partner = me + 1 - 2 * column
    has_ym, has_yp = row > 0, row < GH - 1
    has_zm, has_zp = frame > 0, frame < frames - 1
    ym, yp, zm, zp = me - GW, me + GW, me - per_frame, me + per_frame
    scale = 1.0 / math.sqrt(HD)
    scale2 = scale * math.log2(math.e)
    bf16, f32 = jnp.bfloat16, jnp.float32

    def rows(slot):
        return pl.ds(slot * tok, tok)

    def table(kind, j):
        if kind in (QD_LO, QD_HI):
            low = kind == QD_LO
            return (
                qd.at[j, rows(1), :],
                qd.at[j, rows(0 if low else 2), :],
                yp if low else ym,
                has_yp if low else has_ym,
                has_ym if low else has_yp,
            )
        if kind in (KV_LO, KV_HI):
            low = kind == KV_LO
            return (
                kv.at[j, rows(1), :],
                kv.at[j, rows(0 if low else 2), :],
                zp if low else zm,
                has_zp if low else has_zm,
                has_zm if low else has_zp,
            )
        if kind in (KVP, KVP + 1, KVP + 2):
            d = kind - KVP
            there = (has_zm, None, has_zp)[d]
            return (kv.at[j, rows(d), :], kv.at[j, rows(3 + d), :], partner, there, there)
        if kind in (DKV, DKV1, DKV2):
            d = (DKV, DKV1, DKV2).index(kind)
            return (dkv_out.at[j, d], dkv_in.at[j, d], partner, None, None)
        if kind in (DZ_LO, DZ_HI):
            low = kind == DZ_LO
            return (
                dz_out.at[j, 1 if low else 0],
                dz_in.at[j, 0 if low else 1],
                zp if low else zm,
                has_zp if low else has_zm,
                has_zm if low else has_zp,
            )
        low = kind in (ST_LO, FIN_LO, OQ_LO)
        if kind in (ST_LO, ST_HI):
            source, target = st.at[j, 2 if low else 0], stin.at[j, 0 if low else 1]
        elif kind in (FIN_LO, FIN_HI):
            source, target = fin.at[j, 1], fin.at[j, 0 if low else 2]
        else:
            source, target = oq_out.at[j, 1 if low else 0], oq_in.at[j, 0 if low else 1]
        return (
            source,
            target,
            yp if low else ym,
            has_yp if low else has_ym,
            has_ym if low else has_yp,
        )

    def copy_of(kind, j):
        source, target, device, sent, received = table(kind, j)
        copy = pltpu.make_async_remote_copy(
            src_ref=source,
            dst_ref=target,
            send_sem=send_sem.at[kind, j],
            recv_sem=recv_sem.at[kind, j],
            device_id={"tile": device},
            device_id_type=MESH,
        )
        return copy, sent, received

    def guarded(condition, action):
        if condition is None:
            action()
        else:
            pl.when(condition)(action)

    def send(kind, j):
        copy, sent, _ = copy_of(kind, j)
        guarded(sent, copy.start)

    def arrive(kind, j):
        copy, _, received = copy_of(kind, j)
        guarded(received, copy.wait_recv)

    def sent_off(kind, j):
        copy, sent, _ = copy_of(kind, j)
        guarded(sent, copy.wait_send)

    def start_load(j, _):
        start = pl.multiple_of(j * HD, HD)
        for which, ref, buffer, lane in (
            (0, g_hbm, qd, 0),
            (0, q_hbm, qd, HD),
            (1, v_hbm, kv, 0),
            (1, k_hbm, kv, HD),
        ):
            pltpu.make_async_copy(
                ref.at[:, pl.ds(start, HD)],
                buffer.at[j, rows(1), pl.ds(lane, HD)],
                load_sem.at[which, j],
            ).start()
        return 0

    lax.fori_loop(0, heads, start_load, 0)
    kvt[2 * HD :, :] = jnp.ones((ONES, 6 * tok), bf16)

    def blank(j, _):
        for missing, slot in ((row == 0, 0), (row == GH - 1, 2)):
            @pl.when(missing)
            def _():
                side = slot // 2
                qd[j, rows(slot), :] = jnp.zeros((tok, 2 * HD), bf16)
                stin[j, side] = jnp.concatenate(
                    [jnp.full((1, tok), NEG, f32), jnp.zeros((7, tok), f32)], axis=0
                )
                fin[j, slot] = jnp.zeros((8, tok), f32)
                oq_in[j, side] = jnp.zeros((2 * HD, tok), bf16)

        for missing, slot in ((frame == 0, 0), (frame == frames - 1, 2)):
            @pl.when(missing)
            def _():
                kv[j, rows(slot), :] = jnp.zeros((tok, 2 * HD), bf16)
                kv[j, rows(3 + slot), :] = jnp.zeros((tok, 2 * HD), bf16)
                dz_in[j, slot // 2] = jnp.zeros((tok, 2 * HD), bf16)

        return 0

    barrier = pltpu.get_barrier_semaphore()

    def greet(device):
        pl.semaphore_signal(barrier, inc=1, device_id={"tile": device}, device_id_type=MESH)

    greet(partner)
    for there, device in ((has_ym, ym), (has_yp, yp), (has_zm, zm), (has_zp, zp)):
        pl.when(there)(functools.partial(greet, device))
    lax.fori_loop(0, heads, blank, 0)
    peers = sum(jnp.where(there, 1, 0) for there in (has_ym, has_yp, has_zm, has_zp))
    pl.semaphore_wait(barrier, 1 + peers)

    def send_own(j, _):
        for which, buffer in ((1, kv), (0, qd)):
            own = buffer.at[j, rows(1), :]
            pltpu.make_async_copy(own, own, load_sem.at[which, j]).wait()
            for kind in ((KV_LO, KV_HI, KVP + 1), (QD_LO, QD_HI))[1 - which]:
                send(kind, j)
        return 0

    lax.fori_loop(0, min(AHEAD, heads), send_own, 0)

    def relay(j):
        for kind, onward in ((KV_LO, KVP), (KV_HI, KVP + 2)):
            arrive(kind, j)
            send(onward, j)

    relay(0)

    def prepare(j):
        for kind in (KVP, KVP + 1, KVP + 2, QD_LO, QD_HI):
            arrive(kind, j)
        for kt in range(6):
            kvt[: 2 * HD, rows(kt)] = kv[j, rows(kt), :].T

    def forward(j, s):
        ring = lax.rem(j, 2)
        qrows = pl.ds(pl.multiple_of(s * tok, tok), tok)
        tile = me + (s - 1) * GW
        near = row + s - 1
        exists = jnp.where((near >= 0) & (near < GH), 1, 0)
        tile = jnp.where(exists == 1, tile, me)
        drops = []
        for kt in range(6):
            across = 1 if kt < 3 else 2 - 2 * column
            flag = mask_ref[tile, kt % 3 * 9 + (2 - s) * 3 + across] * exists
            drops.append((1 - flag).astype(f32))
        query = qd[j, qrows, HD:]
        grad = qd[j, qrows, :HD]
        top = jnp.full((1, tok), NEG, f32)
        for kt in range(6):
            block = mm(kv[j, rows(kt), HD:], query, NT)
            scores[rows(kt), :] = block
            peak = jnp.max(block, axis=0, keepdims=True)
            top = jnp.maximum(top, peak * scale2 + drops[kt] * NEG)
            slopes[rows(kt), :] = mm(kv[j, rows(kt), :HD], grad, NT)
        for kt in range(6):
            limits[kt : kt + 1, :] = top + drops[kt] * BIG
        ecols = pl.ds(pl.multiple_of(s * 2 * tok, tok), tok)
        fcols = pl.ds(pl.multiple_of((s * 2 + 1) * tok, tok), tok)

        def weigh(kt, _):
            krows = pl.ds(pl.multiple_of(kt * tok, tok), tok)
            weight = jnp.exp2(scores[krows, :] * scale2 - limits[pl.ds(kt, 1), :])
            ef[ring, krows, ecols] = weight.astype(bf16)
            ef[ring, krows, fcols] = (weight * slopes[krows, :]).astype(bf16)
            return 0

        lax.fori_loop(0, 6, weigh, 0)
        ovk[j, s, :ESUM, :] = mm(kvt[...], ef[ring, :, ecols])
        ovk[j, s, ESUM:, :] = mm(kvt[HD:, :], ef[ring, :, fcols])
        st[j, s, 0:1, :] = top
        st[j, s, 1:2, :] = ovk[j, s, 2 * HD : 2 * HD + 1, :]
        st[j, s, 2:3, :] = ovk[j, s, ESUM + HD : ESUM + HD + 1, :]

    def combine(j):
        arrive(ST_LO, j)
        arrive(ST_HI, j)
        parts = (stin.at[j, 0], st.at[j, 1], stin.at[j, 1])
        tops = [part[0:1, :] for part in parts]
        top = jnp.maximum(jnp.maximum(tops[0], tops[1]), tops[2])
        shares = [jnp.exp2(one - top) for one in tops]
        total = sum(share * part[1:2, :] for share, part in zip(shares, parts))
        moment = sum(share * part[2:3, :] for share, part in zip(shares, parts))
        inverse = 1.0 / total
        fin[j, 1, 0:1, :] = top
        fin[j, 1, 1:2, :] = inverse
        fin[j, 1, 2:3, :] = moment * inverse
        send(FIN_LO, j)
        send(FIN_HI, j)

    def backward(j):
        ring = lax.rem(j, 2)
        arrive(FIN_LO, j)
        arrive(FIN_HI, j)
        for s in (0, 2, 1):
            share = jnp.exp2(st[j, s, 0:1, :] - fin[j, s, 0:1, :]) * fin[j, s, 1:2, :]
            delta = fin[j, s, 2:3, :]
            scaled = share * scale
            output = ovk[j, s, :HD, :] * share
            grad_query = (ovk[j, s, ESUM : ESUM + HD, :] - delta * ovk[j, s, HD : 2 * HD, :]) * scaled
            if s == 1:
                ovk[j, s, :HD, :] = output
                ovk[j, s, HD : 2 * HD, :] = grad_query
            else:
                oq_out[j, s // 2, :HD, :] = output.astype(bf16)
                oq_out[j, s // 2, HD:, :] = grad_query.astype(bf16)
                send(OQ_HI if s == 0 else OQ_LO, j)
            flipped = qd[j, rows(s), :].astype(f32).T
            ecols = pl.ds(s * 2 * tok, tok)
            fcols = pl.ds((s * 2 + 1) * tok, tok)
            wt[:HD, ecols] = (flipped[:HD] * share).astype(bf16)
            wt[HD:, ecols] = (flipped[HD:] * (-scaled * delta)).astype(bf16)
            wt[:HD, fcols] = jnp.zeros((HD, tok), bf16)
            wt[HD:, fcols] = (flipped[HD:] * scaled).astype(bf16)
        for kt in (3, 5, 0, 2, 4, 1):
            part = mm(ef[ring, rows(kt), :], wt[...], NT)
            if kt < 3:
                dkv_own[j, kt] = part
            else:
                dkv_out[j, kt - 3] = part.astype(bf16)
                send((DKV, DKV1, DKV2)[kt - 3], j)
            if kt == 5 and heads > 1:
                pl.when(j == heads - 1)(functools.partial(hand_back, heads - 2))
            if kt == 2:
                pl.when(j == heads - 1)(functools.partial(hand_back, heads - 1))

    def hand_back(j):
        arrive(DKV, j)
        arrive(DKV2, j)
        for d, kind in ((0, DZ_HI), (2, DZ_LO)):
            dz_out[j, d // 2] = (dkv_own[j, d] + dkv_in[j, d].astype(f32)).astype(bf16)
            send(kind, j)

    def finish(j):
        for kind in (OQ_LO, OQ_HI, DKV1, DZ_LO, DZ_HI):
            arrive(kind, j)
        both = ovk[j, 1, : 2 * HD, :] + oq_in[j, 0].astype(f32) + oq_in[j, 1].astype(f32)
        both = both.T
        result[j, 0] = both[:, :HD].astype(bf16)
        result[j, 1] = both[:, HD:].astype(bf16)
        both = dkv_own[j, 1] + dkv_in[j, 1].astype(f32)
        both = both + dz_in[j, 0].astype(f32) + dz_in[j, 1].astype(f32)
        result[j, 2] = both[:, HD:].astype(bf16)
        result[j, 3] = both[:, :HD].astype(bf16)
        for n in range(4):
            output(j, n).start()

    def output(j, n):
        cols = pl.ds(pl.multiple_of(j * HD, HD), HD)
        target = (att_ref, gq_ref, gk_ref, gv_ref)[n].at[:, cols]
        return pltpu.make_async_copy(result.at[j, n], target, out_sem.at[j, n])

    def step(i, _):
        pl.when(i < heads)(functools.partial(prepare, i))

        def inner(turn, _):
            s = lax.rem(2 * turn, 3)

            @pl.when(i < heads)
            def _():
                forward(i, s)

                @pl.when(turn == 0)
                def _():
                    send(ST_HI, i)

                @pl.when(turn == 1)
                def _():
                    send(ST_LO, i)

                @pl.when((turn == 0) & (i + 1 < heads))
                def _():
                    relay(i + 1)

                @pl.when((turn == 0) & (i + AHEAD < heads))
                def _():
                    send_own(i + AHEAD, 0)

                pl.when((turn == 1) & (i >= 2))(functools.partial(hand_back, i - 2))

            pl.when((turn == 0) & (i >= 3))(functools.partial(finish, i - 3))
            return 0

        lax.fori_loop(0, 3, inner, 0)
        pl.when(i < heads)(functools.partial(combine, i))
        pl.when((i >= 1) & (i <= heads))(functools.partial(backward, i - 1))
        return 0

    lax.fori_loop(0, heads + 3, step, 0)

    def drain(j, _):
        for kind in range(KINDS):
            sent_off(kind, j)
        for n in range(4):
            output(j, n).wait()
        return 0

    lax.fori_loop(0, heads, drain, 0)


def put(*refs):
    sources, targets, (held, take_sem, give_sem) = refs[:4], refs[4:8], refs[8:]
    takes = [pltpu.make_async_copy(sources[n], held.at[n], take_sem.at[n]) for n in range(4)]
    gives = [pltpu.make_async_copy(held.at[n], targets[n], give_sem.at[n]) for n in range(4)]
    for take in takes:
        take.start()
    for take, give in zip(takes, gives):
        take.wait()
        give.start()
    for give in gives:
        give.wait()


def on_device(queries, keys, values, reward_grad, window_mask):
    tok, width = queries.shape
    heads = width // HD
    frames = lax.axis_size("tile") // (GH * GW)
    bf16, f32 = jnp.bfloat16, jnp.float32
    hbm = pl.BlockSpec(memory_space=pltpu.MemorySpace.HBM)
    results = pl.pallas_call(
        functools.partial(kernel, heads, tok, frames),
        out_shape=[jax.ShapeDtypeStruct((tok, width), bf16)] * 4,
        in_specs=[pl.BlockSpec(memory_space=pltpu.SMEM), hbm, hbm, hbm, hbm],
        out_specs=[hbm] * 4,
        scratch_shapes=[
            pltpu.VMEM((heads, 3 * tok, 2 * HD), bf16),
            pltpu.VMEM((heads, 6 * tok, 2 * HD), bf16),
            pltpu.VMEM((ESUM, 6 * tok), bf16),
            pltpu.VMEM((6 * tok, tok), f32),
            pltpu.VMEM((6 * tok, tok), f32),
            pltpu.VMEM((8, tok), f32),
            pltpu.VMEM((2, 6 * tok, 6 * tok), bf16),
            pltpu.VMEM((heads, 3, 2 * ESUM - HD, tok), f32),
            pltpu.VMEM((2 * HD, 6 * tok), bf16),
            pltpu.VMEM((heads, 3, 8, tok), f32),
            pltpu.VMEM((heads, 2, 8, tok), f32),
            pltpu.VMEM((heads, 3, 8, tok), f32),
            pltpu.VMEM((heads, 2, 2 * HD, tok), bf16),
            pltpu.VMEM((heads, 2, 2 * HD, tok), bf16),
            pltpu.VMEM((heads, 3, tok, 2 * HD), f32),
            pltpu.VMEM((heads, 3, tok, 2 * HD), bf16),
            pltpu.VMEM((heads, 3, tok, 2 * HD), bf16),
            pltpu.VMEM((heads, 2, tok, 2 * HD), bf16),
            pltpu.VMEM((heads, 2, tok, 2 * HD), bf16),
            pltpu.VMEM((heads, 4, tok, HD), bf16),
            pltpu.SemaphoreType.DMA((2, heads)),
            pltpu.SemaphoreType.DMA((heads, 4)),
            pltpu.SemaphoreType.DMA((KINDS, heads)),
            pltpu.SemaphoreType.DMA((KINDS, heads)),
        ],
        compiler_params=pltpu.CompilerParams(
            collective_id=0, has_side_effects=True, vmem_limit_bytes=60 * 1024 * 1024
        ),
    )(window_mask, queries, keys, values, reward_grad)
    return pl.pallas_call(
        put,
        out_shape=[jax.ShapeDtypeStruct((tok, width), bf16)] * 4,
        in_specs=[hbm] * 4,
        out_specs=[hbm] * 4,
        scratch_shapes=[
            pltpu.VMEM((4, tok, width), bf16),
            pltpu.SemaphoreType.DMA((4,)),
            pltpu.SemaphoreType.DMA((4,)),
        ],
    )(*results)


def solution(mesh):
    return jax.shard_map(
        on_device,
        mesh=mesh,
        in_specs=(P("tile", "head"), P("tile", "head"), P("tile", "head"), P("tile", "head"), P()),
        out_specs=(P("tile", "head"), P("tile", "head"), P("tile", "head"), P("tile", "head")),
        check_vma=False,
    )
```

```python
import functools
import math

import jax
import jax.numpy as jnp
from jax import lax
from jax.experimental import pallas as pl
from jax.experimental.pallas import tpu as pltpu
from jax.sharding import PartitionSpec as P

HD = 128
GH = 4
GW = 2


QD_LO, QD_HI, KV_LO, KV_HI, KVP = 0, 1, 2, 3, 4
ST_LO, ST_HI, FIN_LO, FIN_HI, OQ_LO, OQ_HI, DKV, DZ_LO, DZ_HI = 7, 8, 9, 10, 11, 12, 13, 14, 15
DKV1, DKV2 = 16, 17
KINDS = 18

AHEAD = 2

ONES = 16
ESUM = 2 * HD + ONES

NT = (((1,), (1,)), ((), ()))
NEG = -1e30
BIG = 3e30
MESH = pl.DeviceIdType.MESH


def mm(left, right, dims=(((1,), (0,)), ((), ()))):
    return lax.dot_general(left, right, dims, preferred_element_type=jnp.float32)


def kernel(
    heads,
    tok,
    frames,
    mask_ref,
    q_hbm,
    k_hbm,
    v_hbm,
    g_hbm,
    att_ref,
    gq_ref,
    gk_ref,
    gv_ref,
    qd,
    kv,
    kvt,
    scores,
    slopes,
    first_top,
    ef,
    ovk,
    wt,
    st,
    stin,
    fin,
    oq_out,
    oq_in,
    dkv_own,
    dkv_out,
    dkv_in,
    dz_out,
    dz_in,
    result,
    load_sem,
    out_sem,
    send_sem,
    recv_sem,
):
    me = lax.axis_index("tile")
    per_frame = GH * GW
    frame = me // per_frame
    row = me // GW % GH
    column = me % GW
    partner = me + 1 - 2 * column
    has_ym, has_yp = row > 0, row < GH - 1
    has_zm, has_zp = frame > 0, frame < frames - 1
    ym, yp, zm, zp = me - GW, me + GW, me - per_frame, me + per_frame
    scale = 1.0 / math.sqrt(HD)
    scale2 = scale * math.log2(math.e)
    bf16, f32 = jnp.bfloat16, jnp.float32

    def rows(slot):
        return pl.ds(slot * tok, tok)

    def table(kind, j):
        if kind in (QD_LO, QD_HI):
            low = kind == QD_LO
            return (
                qd.at[j, rows(1), :],
                qd.at[j, rows(0 if low else 2), :],
                yp if low else ym,
                has_yp if low else has_ym,
                has_ym if low else has_yp,
            )
        if kind in (KV_LO, KV_HI):
            low = kind == KV_LO
            return (
                kv.at[j, rows(1), :],
                kv.at[j, rows(0 if low else 2), :],
                zp if low else zm,
                has_zp if low else has_zm,
                has_zm if low else has_zp,
            )
        if kind in (KVP, KVP + 1, KVP + 2):
            d = kind - KVP
            there = (has_zm, None, has_zp)[d]
            return (kv.at[j, rows(d), :], kv.at[j, rows(3 + d), :], partner, there, there)
        if kind in (DKV, DKV1, DKV2):
            d = (DKV, DKV1, DKV2).index(kind)
            return (dkv_out.at[j, d], dkv_in.at[j, d], partner, None, None)
        if kind in (DZ_LO, DZ_HI):
            low = kind == DZ_LO
            return (
                dz_out.at[j, 1 if low else 0],
                dz_in.at[j, 0 if low else 1],
                zp if low else zm,
                has_zp if low else has_zm,
                has_zm if low else has_zp,
            )
        low = kind in (ST_LO, FIN_LO, OQ_LO)
        if kind in (ST_LO, ST_HI):
            source, target = st.at[j, 2 if low else 0], stin.at[j, 0 if low else 1]
        elif kind in (FIN_LO, FIN_HI):
            source, target = fin.at[j, 1], fin.at[j, 0 if low else 2]
        else:
            source, target = oq_out.at[j, 1 if low else 0], oq_in.at[j, 0 if low else 1]
        return (
            source,
            target,
            yp if low else ym,
            has_yp if low else has_ym,
            has_ym if low else has_yp,
        )

    def copy_of(kind, j):
        source, target, device, sent, received = table(kind, j)
        copy = pltpu.make_async_remote_copy(
            src_ref=source,
            dst_ref=target,
            send_sem=send_sem.at[kind, j],
            recv_sem=recv_sem.at[kind, j],
            device_id={"tile": device},
            device_id_type=MESH,
        )
        return copy, sent, received

    def guarded(condition, action):
        if condition is None:
            action()
        else:
            pl.when(condition)(action)

    def send(kind, j):
        copy, sent, _ = copy_of(kind, j)
        guarded(sent, copy.start)

    def arrive(kind, j):
        copy, _, received = copy_of(kind, j)
        guarded(received, copy.wait_recv)

    def sent_off(kind, j):
        copy, sent, _ = copy_of(kind, j)
        guarded(sent, copy.wait_send)

    def start_load(j, _):
        start = pl.multiple_of(j * HD, HD)
        for which, ref, buffer, lane in (
            (0, g_hbm, qd, 0),
            (0, q_hbm, qd, HD),
            (1, v_hbm, kv, 0),
            (1, k_hbm, kv, HD),
        ):
            pltpu.make_async_copy(
                ref.at[:, pl.ds(start, HD)],
                buffer.at[j, rows(1), pl.ds(lane, HD)],
                load_sem.at[which, j],
            ).start()
        return 0

    lax.fori_loop(0, heads, start_load, 0)
    kvt[2 * HD :, :] = jnp.ones((ONES, 6 * tok), bf16)

    def blank(j, _):
        for missing, slot in ((row == 0, 0), (row == GH - 1, 2)):
            @pl.when(missing)
            def _():
                side = slot // 2
                qd[j, rows(slot), :] = jnp.zeros((tok, 2 * HD), bf16)
                stin[j, side] = jnp.concatenate(
                    [jnp.full((1, tok), NEG, f32), jnp.zeros((7, tok), f32)], axis=0
                )
                fin[j, slot] = jnp.zeros((8, tok), f32)
                oq_in[j, side] = jnp.zeros((2 * HD, tok), bf16)

        for missing, slot in ((frame == 0, 0), (frame == frames - 1, 2)):
            @pl.when(missing)
            def _():
                kv[j, rows(slot), :] = jnp.zeros((tok, 2 * HD), bf16)
                kv[j, rows(3 + slot), :] = jnp.zeros((tok, 2 * HD), bf16)
                dz_in[j, slot // 2] = jnp.zeros((tok, 2 * HD), bf16)

        return 0

    barrier = pltpu.get_barrier_semaphore()

    def greet(device):
        pl.semaphore_signal(barrier, inc=1, device_id={"tile": device}, device_id_type=MESH)

    greet(partner)
    for there, device in ((has_ym, ym), (has_yp, yp), (has_zm, zm), (has_zp, zp)):
        pl.when(there)(functools.partial(greet, device))
    lax.fori_loop(0, heads, blank, 0)
    peers = sum(jnp.where(there, 1, 0) for there in (has_ym, has_yp, has_zm, has_zp))
    pl.semaphore_wait(barrier, 1 + peers)

    def send_own(j, _):
        for which, buffer in ((1, kv), (0, qd)):
            own = buffer.at[j, rows(1), :]
            pltpu.make_async_copy(own, own, load_sem.at[which, j]).wait()
            for kind in ((KV_LO, KV_HI, KVP + 1), (QD_LO, QD_HI))[1 - which]:
                send(kind, j)
        return 0

    lax.fori_loop(0, min(AHEAD, heads), send_own, 0)

    def relay(j):
        for kind, onward in ((KV_LO, KVP), (KV_HI, KVP + 2)):
            arrive(kind, j)
            send(onward, j)

    relay(0)

    def forward(j, hooks):
        for kind in (KVP, KVP + 1, KVP + 2, QD_LO, QD_HI):
            arrive(kind, j)
        ring = lax.rem(j, 2)
        order = (0, 2, 1)

        def dropped(s):
            near = row + s - 1
            exists = jnp.where((near >= 0) & (near < GH), 1, 0)
            tile = jnp.where(exists == 1, me + (s - 1) * GW, me)
            drops = []
            for kt in range(6):
                across = 1 if kt < 3 else 2 - 2 * column
                flag = mask_ref[tile, kt % 3 * 9 + (2 - s) * 3 + across] * exists
                drops.append((1 - flag).astype(f32))
            return drops

        def score(s, kt, drop, top, held):
            block = mm(kv[j, rows(kt), HD:], qd[j, rows(s), HD:], NT)
            scores[held][rows(kt), :] = block
            slopes[held][rows(kt), :] = mm(kv[j, rows(kt), :HD], qd[j, rows(s), :HD], NT)
            peak = jnp.max(block, axis=0, keepdims=True)
            return jnp.maximum(top, peak * scale2 + drop * NEG)

        empty = jnp.full((1, tok), NEG, f32)

        @pl.when(me >= 0)
        def _():
            drops = dropped(order[0])
            top = empty
            for kt in range(6):
                top = score(order[0], kt, drops[kt], top, 0)
                kvt[: 2 * HD, rows(kt)] = kv[j, rows(kt), :].T
            first_top[0:1, :] = top

        drops = dropped(order[0])
        top = first_top[0:1, :]
        for turn, s in enumerate(order):
            held = turn % 2
            ecols, fcols = pl.ds(s * 2 * tok, tok), pl.ds((s * 2 + 1) * tok, tok)
            later = empty
            if turn < 2:
                next_drops = dropped(order[turn + 1])
            for kt in range(6):
                limit = top + drops[kt] * BIG
                weight = jnp.exp2(scores[held][rows(kt), :] * scale2 - limit)
                ef[ring, rows(kt), ecols] = weight.astype(bf16)
                ef[ring, rows(kt), fcols] = (weight * slopes[held][rows(kt), :]).astype(bf16)
                if turn < 2:
                    later = score(order[turn + 1], kt, next_drops[kt], later, 1 - held)
            ovk[j, s, :ESUM, :] = mm(kvt[...], ef[ring, :, ecols])
            ovk[j, s, ESUM:, :] = mm(kvt[HD:, :], ef[ring, :, fcols])
            st[j, s, 0:1, :] = top
            st[j, s, 1:2, :] = ovk[j, s, 2 * HD : 2 * HD + 1, :]
            st[j, s, 2:3, :] = ovk[j, s, ESUM + HD : ESUM + HD + 1, :]
            hooks[turn]()
            top = later
            if turn < 2:
                drops = next_drops

    def combine(j):
        arrive(ST_LO, j)
        arrive(ST_HI, j)
        parts = (stin.at[j, 0], st.at[j, 1], stin.at[j, 1])
        tops = [part[0:1, :] for part in parts]
        top = jnp.maximum(jnp.maximum(tops[0], tops[1]), tops[2])
        shares = [jnp.exp2(one - top) for one in tops]
        total = sum(share * part[1:2, :] for share, part in zip(shares, parts))
        moment = sum(share * part[2:3, :] for share, part in zip(shares, parts))
        inverse = 1.0 / total
        fin[j, 1, 0:1, :] = top
        fin[j, 1, 1:2, :] = inverse
        fin[j, 1, 2:3, :] = moment * inverse
        send(FIN_LO, j)
        send(FIN_HI, j)

    def backward(last, j):
        ring = lax.rem(j, 2)
        arrive(FIN_LO, j)
        arrive(FIN_HI, j)
        for s in (0, 2, 1):
            share = jnp.exp2(st[j, s, 0:1, :] - fin[j, s, 0:1, :]) * fin[j, s, 1:2, :]
            delta = fin[j, s, 2:3, :]
            scaled = share * scale
            output = ovk[j, s, :HD, :] * share
            grad_query = (ovk[j, s, ESUM : ESUM + HD, :] - delta * ovk[j, s, HD : 2 * HD, :]) * scaled
            if s == 1:
                ovk[j, s, :HD, :] = output
                ovk[j, s, HD : 2 * HD, :] = grad_query
            else:
                oq_out[j, s // 2, :HD, :] = output.astype(bf16)
                oq_out[j, s // 2, HD:, :] = grad_query.astype(bf16)
            flipped = qd[j, rows(s), :].astype(f32).T
            ecols = pl.ds(s * 2 * tok, tok)
            fcols = pl.ds((s * 2 + 1) * tok, tok)
            wt[:HD, ecols] = (flipped[:HD] * share).astype(bf16)
            wt[HD:, ecols] = (flipped[HD:] * (-scaled * delta)).astype(bf16)
            wt[:HD, fcols] = jnp.zeros((HD, tok), bf16)
            wt[HD:, fcols] = (flipped[HD:] * scaled).astype(bf16)
        if last:
            send(OQ_HI, j)
            send(OQ_LO, j)
        for kt in (3, 5, 0, 2, 4, 1):
            part = mm(ef[ring, rows(kt), :], wt[...], NT)
            if kt < 3:
                dkv_own[j, kt] = part
            else:
                dkv_out[j, kt - 3] = part.astype(bf16)
                send((DKV, DKV1, DKV2)[kt - 3], j)
            if last and kt == 2:
                hand_back(heads - 1)
        if not last:
            send(OQ_HI, j)
            send(OQ_LO, j)

    def hand_back(j):
        arrive(DKV, j)
        arrive(DKV2, j)
        for d, kind in ((0, DZ_HI), (2, DZ_LO)):
            dz_out[j, d // 2] = (dkv_own[j, d] + dkv_in[j, d].astype(f32)).astype(bf16)
            send(kind, j)

    def finish(j):
        for kind in (OQ_LO, OQ_HI, DKV1, DZ_LO, DZ_HI):
            arrive(kind, j)
        both = ovk[j, 1, : 2 * HD, :] + oq_in[j, 0].astype(f32) + oq_in[j, 1].astype(f32)
        both = both.T
        result[j, 0] = both[:, :HD].astype(bf16)
        result[j, 1] = both[:, HD:].astype(bf16)
        both = dkv_own[j, 1] + dkv_in[j, 1].astype(f32)
        both = both + dz_in[j, 0].astype(f32) + dz_in[j, 1].astype(f32)
        result[j, 2] = both[:, HD:].astype(bf16)
        result[j, 3] = both[:, :HD].astype(bf16)
        for n in range(4):
            output(j, n).start()

    def output(j, n):
        cols = pl.ds(pl.multiple_of(j * HD, HD), HD)
        target = (att_ref, gq_ref, gk_ref, gv_ref)[n].at[:, cols]
        return pltpu.make_async_copy(result.at[j, n], target, out_sem.at[j, n])

    def step(i, _):
        def first():
            send(ST_HI, i)
            pl.when(i + 1 < heads)(functools.partial(relay, i + 1))

            @pl.when(i + AHEAD < heads)
            def _():
                send_own(i + AHEAD, 0)

            pl.when(i >= 2)(functools.partial(hand_back, i - 2))

        forward(i, (first, functools.partial(send, ST_LO, i), lambda: None))
        pl.when(i >= 3)(functools.partial(finish, i - 3))
        pl.when(i == heads - 1)(functools.partial(combine, i))
        pl.when(i >= 1)(functools.partial(backward, False, i - 1))
        pl.when(i < heads - 1)(functools.partial(combine, i))
        return 0

    lax.fori_loop(0, heads, step, 0)
    if heads > 2:
        finish(heads - 3)
    if heads > 1:
        hand_back(heads - 2)
    backward(True, heads - 1)
    if heads > 1:
        finish(heads - 2)

    def drain(j, _):
        for kind in range(KINDS):
            sent_off(kind, j)
        return 0

    lax.fori_loop(0, heads, drain, 0)
    finish(heads - 1)

    def written(j, _):
        for n in range(4):
            output(j, n).wait()
        return 0

    lax.fori_loop(0, heads, written, 0)


def put(*refs):
    sources, targets, (held, take_sem, give_sem) = refs[:4], refs[4:8], refs[8:]
    takes = [pltpu.make_async_copy(sources[n], held.at[n], take_sem.at[n]) for n in range(4)]
    gives = [pltpu.make_async_copy(held.at[n], targets[n], give_sem.at[n]) for n in range(4)]
    for take in takes:
        take.start()
    for take, give in zip(takes, gives):
        take.wait()
        give.start()
    for give in gives:
        give.wait()


def on_device(queries, keys, values, reward_grad, window_mask):
    tok, width = queries.shape
    heads = width // HD
    frames = lax.axis_size("tile") // (GH * GW)
    bf16, f32 = jnp.bfloat16, jnp.float32
    hbm = pl.BlockSpec(memory_space=pltpu.MemorySpace.HBM)
    results = pl.pallas_call(
        functools.partial(kernel, heads, tok, frames),
        out_shape=[jax.ShapeDtypeStruct((tok, width), bf16)] * 4,
        in_specs=[pl.BlockSpec(memory_space=pltpu.SMEM), hbm, hbm, hbm, hbm],
        out_specs=[hbm] * 4,
        scratch_shapes=[
            pltpu.VMEM((heads, 3 * tok, 2 * HD), bf16),
            pltpu.VMEM((heads, 6 * tok, 2 * HD), bf16),
            pltpu.VMEM((ESUM, 6 * tok), bf16),
            [pltpu.VMEM((6 * tok, tok), f32)] * 2,
            [pltpu.VMEM((6 * tok, tok), f32)] * 2,
            pltpu.VMEM((8, tok), f32),
            pltpu.VMEM((2, 6 * tok, 6 * tok), bf16),
            pltpu.VMEM((heads, 3, 2 * ESUM - HD, tok), f32),
            pltpu.VMEM((2 * HD, 6 * tok), bf16),
            pltpu.VMEM((heads, 3, 8, tok), f32),
            pltpu.VMEM((heads, 2, 8, tok), f32),
            pltpu.VMEM((heads, 3, 8, tok), f32),
            pltpu.VMEM((heads, 2, 2 * HD, tok), bf16),
            pltpu.VMEM((heads, 2, 2 * HD, tok), bf16),
            pltpu.VMEM((heads, 3, tok, 2 * HD), f32),
            pltpu.VMEM((heads, 3, tok, 2 * HD), bf16),
            pltpu.VMEM((heads, 3, tok, 2 * HD), bf16),
            pltpu.VMEM((heads, 2, tok, 2 * HD), bf16),
            pltpu.VMEM((heads, 2, tok, 2 * HD), bf16),
            pltpu.VMEM((heads, 4, tok, HD), bf16),
            pltpu.SemaphoreType.DMA((2, heads)),
            pltpu.SemaphoreType.DMA((heads, 4)),
            pltpu.SemaphoreType.DMA((KINDS, heads)),
            pltpu.SemaphoreType.DMA((KINDS, heads)),
        ],
        compiler_params=pltpu.CompilerParams(
            collective_id=0, has_side_effects=True, vmem_limit_bytes=60 * 1024 * 1024
        ),
    )(window_mask, queries, keys, values, reward_grad)
    return pl.pallas_call(
        put,
        out_shape=[jax.ShapeDtypeStruct((tok, width), bf16)] * 4,
        in_specs=[hbm] * 4,
        out_specs=[hbm] * 4,
        scratch_shapes=[
            pltpu.VMEM((4, tok, width), bf16),
            pltpu.SemaphoreType.DMA((4,)),
            pltpu.SemaphoreType.DMA((4,)),
        ],
    )(*results)


def solution(mesh):
    return jax.shard_map(
        on_device,
        mesh=mesh,
        in_specs=(P("tile", "head"), P("tile", "head"), P("tile", "head"), P("tile", "head"), P()),
        out_specs=(P("tile", "head"), P("tile", "head"), P("tile", "head"), P("tile", "head")),
        check_vma=False,
    )
```

```python
import functools
import math

import jax
import jax.numpy as jnp
from jax import lax
from jax.experimental import pallas as pl
from jax.experimental.pallas import tpu as pltpu
from jax.sharding import PartitionSpec as P

HD = 128
GH = 4
GW = 2


QD_LO, QD_HI, KV_LO, KV_HI, KVP = 0, 1, 2, 3, 4
ST_LO, ST_HI, FIN_LO, FIN_HI, OQ_LO, OQ_HI, DKV, DZ_LO, DZ_HI = 7, 8, 9, 10, 11, 12, 13, 14, 15
DKV1, DKV2 = 16, 17
KINDS = 18

AHEAD = 2

ONES = 16
ESUM = 2 * HD + ONES

NT = (((1,), (1,)), ((), ()))
NEG = -1e30
BIG = 3e30
MESH = pl.DeviceIdType.MESH


def mm(left, right, dims=(((1,), (0,)), ((), ()))):
    return lax.dot_general(left, right, dims, preferred_element_type=jnp.float32)


def kernel(
    heads,
    tok,
    frames,
    mask_ref,
    q_hbm,
    k_hbm,
    v_hbm,
    g_hbm,
    att_ref,
    gq_ref,
    gk_ref,
    gv_ref,
    qd,
    kv,
    kvt,
    scores,
    slopes,
    first_top,
    ef,
    ovk,
    wt,
    st,
    stin,
    fin,
    oq_out,
    oq_in,
    dkv_own,
    dkv_out,
    dkv_in,
    dz_out,
    dz_in,
    result,
    load_sem,
    out_sem,
    send_sem,
    recv_sem,
):
    me = lax.axis_index("tile")
    per_frame = GH * GW
    frame = me // per_frame
    row = me // GW % GH
    column = me % GW
    partner = me + 1 - 2 * column
    has_ym, has_yp = row > 0, row < GH - 1
    has_zm, has_zp = frame > 0, frame < frames - 1
    ym, yp, zm, zp = me - GW, me + GW, me - per_frame, me + per_frame
    scale = 1.0 / math.sqrt(HD)
    scale2 = scale * math.log2(math.e)
    bf16, f32 = jnp.bfloat16, jnp.float32

    def rows(slot):
        return pl.ds(slot * tok, tok)

    def table(kind, j):
        if kind in (QD_LO, QD_HI):
            low = kind == QD_LO
            return (
                qd.at[j, rows(1), :],
                qd.at[j, rows(0 if low else 2), :],
                yp if low else ym,
                has_yp if low else has_ym,
                has_ym if low else has_yp,
            )
        if kind in (KV_LO, KV_HI):
            low = kind == KV_LO
            return (
                kv.at[j, rows(1), :],
                kv.at[j, rows(0 if low else 2), :],
                zp if low else zm,
                has_zp if low else has_zm,
                has_zm if low else has_zp,
            )
        if kind in (KVP, KVP + 1, KVP + 2):
            d = kind - KVP
            there = (has_zm, None, has_zp)[d]
            return (kv.at[j, rows(d), :], kv.at[j, rows(3 + d), :], partner, there, there)
        if kind in (DKV, DKV1, DKV2):
            d = (DKV, DKV1, DKV2).index(kind)
            return (dkv_out.at[j, d], dkv_in.at[j, d], partner, None, None)
        if kind in (DZ_LO, DZ_HI):
            low = kind == DZ_LO
            return (
                dz_out.at[j, 1 if low else 0],
                dz_in.at[j, 0 if low else 1],
                zp if low else zm,
                has_zp if low else has_zm,
                has_zm if low else has_zp,
            )
        low = kind in (ST_LO, FIN_LO, OQ_LO)
        if kind in (ST_LO, ST_HI):
            source, target = st.at[j, 2 if low else 0], stin.at[j, 0 if low else 1]
        elif kind in (FIN_LO, FIN_HI):
            source, target = fin.at[j, 1], fin.at[j, 0 if low else 2]
        else:
            source, target = oq_out.at[j, 1 if low else 0], oq_in.at[j, 0 if low else 1]
        return (
            source,
            target,
            yp if low else ym,
            has_yp if low else has_ym,
            has_ym if low else has_yp,
        )

    def copy_of(kind, j):
        source, target, device, sent, received = table(kind, j)
        copy = pltpu.make_async_remote_copy(
            src_ref=source,
            dst_ref=target,
            send_sem=send_sem.at[kind, j],
            recv_sem=recv_sem.at[kind, j],
            device_id={"tile": device},
            device_id_type=MESH,
        )
        return copy, sent, received

    def guarded(condition, action):
        if condition is None:
            action()
        else:
            pl.when(condition)(action)

    def send(kind, j):
        copy, sent, _ = copy_of(kind, j)
        guarded(sent, copy.start)

    def arrive(kind, j):
        copy, _, received = copy_of(kind, j)
        guarded(received, copy.wait_recv)

    def sent_off(kind, j):
        copy, sent, _ = copy_of(kind, j)
        guarded(sent, copy.wait_send)

    barrier = pltpu.get_barrier_semaphore()

    def greet(device):
        pl.semaphore_signal(barrier, inc=1, device_id={"tile": device}, device_id_type=MESH)

    greet(partner)
    for there, device in ((has_ym, ym), (has_yp, yp), (has_zm, zm), (has_zp, zp)):
        pl.when(there)(functools.partial(greet, device))

    def start_load(j, _):
        start = pl.multiple_of(j * HD, HD)
        for which, ref, buffer, lane in (
            (0, g_hbm, qd, 0),
            (0, q_hbm, qd, HD),
            (1, v_hbm, kv, 0),
            (1, k_hbm, kv, HD),
        ):
            pltpu.make_async_copy(
                ref.at[:, pl.ds(start, HD)],
                buffer.at[j, rows(1), pl.ds(lane, HD)],
                load_sem.at[which, j],
            ).start()
        return 0

    lax.fori_loop(0, heads, start_load, 0)
    kvt[2 * HD :, :] = jnp.ones((ONES, 6 * tok), bf16)

    def blank(j, _):
        for missing, slot in ((row == 0, 0), (row == GH - 1, 2)):
            @pl.when(missing)
            def _():
                side = slot // 2
                qd[j, rows(slot), :] = jnp.zeros((tok, 2 * HD), bf16)
                stin[j, side] = jnp.concatenate(
                    [jnp.full((1, tok), NEG, f32), jnp.zeros((7, tok), f32)], axis=0
                )
                fin[j, slot] = jnp.zeros((8, tok), f32)
                oq_in[j, side] = jnp.zeros((2 * HD, tok), bf16)

        for missing, slot in ((frame == 0, 0), (frame == frames - 1, 2)):
            @pl.when(missing)
            def _():
                kv[j, rows(slot), :] = jnp.zeros((tok, 2 * HD), bf16)
                kv[j, rows(3 + slot), :] = jnp.zeros((tok, 2 * HD), bf16)
                dz_in[j, slot // 2] = jnp.zeros((tok, 2 * HD), bf16)

        return 0

    lax.fori_loop(0, heads, blank, 0)
    peers = sum(jnp.where(there, 1, 0) for there in (has_ym, has_yp, has_zm, has_zp))
    pl.semaphore_wait(barrier, 1 + peers)

    def send_own(which, j):
        buffer = (qd, kv)[which]
        own = buffer.at[j, rows(1), :]
        pltpu.make_async_copy(own, own, load_sem.at[which, j]).wait()
        for kind in ((QD_LO, QD_HI), (KV_LO, KV_HI, KVP + 1))[which]:
            send(kind, j)

    def open_with(j, _):
        send_own(1, j)
        send_own(0, j)
        return 0

    lax.fori_loop(0, min(AHEAD, heads), open_with, 0)

    def relay(j):
        for kind, onward in ((KV_LO, KVP), (KV_HI, KVP + 2)):
            arrive(kind, j)
            send(onward, j)

    relay(0)

    def forward(j, hooks):
        for kind in (KVP, KVP + 1, KVP + 2, QD_LO, QD_HI):
            arrive(kind, j)
        ring = lax.rem(j, 2)
        order = (0, 2, 1)

        def dropped(s):
            near = row + s - 1
            exists = jnp.where((near >= 0) & (near < GH), 1, 0)
            tile = jnp.where(exists == 1, me + (s - 1) * GW, me)
            drops = []
            for kt in range(6):
                across = 1 if kt < 3 else 2 - 2 * column
                flag = mask_ref[tile, kt % 3 * 9 + (2 - s) * 3 + across] * exists
                drops.append((1 - flag).astype(f32))
            return drops

        def score(s, kt, drop, top, held):
            block = mm(kv[j, rows(kt), HD:], qd[j, rows(s), HD:], NT)
            scores[held][rows(kt), :] = block
            slopes[held][rows(kt), :] = mm(kv[j, rows(kt), :HD], qd[j, rows(s), :HD], NT)
            peak = jnp.max(block, axis=0, keepdims=True)
            return jnp.maximum(top, peak * scale2 + drop * NEG)

        empty = jnp.full((1, tok), NEG, f32)

        @pl.when(me >= 0)
        def _():
            drops = dropped(order[0])
            top = empty
            for kt in range(6):
                top = score(order[0], kt, drops[kt], top, 0)
                kvt[: 2 * HD, rows(kt)] = kv[j, rows(kt), :].T
            first_top[0:1, :] = top

        drops = dropped(order[0])
        top = first_top[0:1, :]
        for turn, s in enumerate(order):
            held = turn % 2
            ecols, fcols = pl.ds(s * 2 * tok, tok), pl.ds((s * 2 + 1) * tok, tok)
            later = empty
            if turn < 2:
                next_drops = dropped(order[turn + 1])
            for kt in range(6):
                limit = top + drops[kt] * BIG
                weight = jnp.exp2(scores[held][rows(kt), :] * scale2 - limit)
                ef[ring, rows(kt), ecols] = weight.astype(bf16)
                ef[ring, rows(kt), fcols] = (weight * slopes[held][rows(kt), :]).astype(bf16)
                if turn < 2:
                    later = score(order[turn + 1], kt, next_drops[kt], later, 1 - held)
            ovk[j, s, :ESUM, :] = mm(kvt[...], ef[ring, :, ecols])
            ovk[j, s, ESUM:, :] = mm(kvt[HD:, :], ef[ring, :, fcols])
            st[j, s, 0:1, :] = top
            st[j, s, 1:2, :] = ovk[j, s, 2 * HD : 2 * HD + 1, :]
            st[j, s, 2:3, :] = ovk[j, s, ESUM + HD : ESUM + HD + 1, :]
            hooks[turn]()
            top = later
            if turn < 2:
                drops = next_drops

    def combine(j):
        arrive(ST_LO, j)
        arrive(ST_HI, j)
        parts = (stin.at[j, 0], st.at[j, 1], stin.at[j, 1])
        tops = [part[0:1, :] for part in parts]
        top = jnp.maximum(jnp.maximum(tops[0], tops[1]), tops[2])
        shares = [jnp.exp2(one - top) for one in tops]
        total = sum(share * part[1:2, :] for share, part in zip(shares, parts))
        moment = sum(share * part[2:3, :] for share, part in zip(shares, parts))
        inverse = 1.0 / total
        fin[j, 1, 0:1, :] = top
        fin[j, 1, 1:2, :] = inverse
        fin[j, 1, 2:3, :] = moment * inverse
        send(FIN_LO, j)
        send(FIN_HI, j)

    def backward(last, j):
        ring = lax.rem(j, 2)
        arrive(FIN_LO, j)
        arrive(FIN_HI, j)
        for s in (0, 2, 1):
            share = jnp.exp2(st[j, s, 0:1, :] - fin[j, s, 0:1, :]) * fin[j, s, 1:2, :]
            delta = fin[j, s, 2:3, :]
            scaled = share * scale
            output = ovk[j, s, :HD, :] * share
            grad_query = (ovk[j, s, ESUM : ESUM + HD, :] - delta * ovk[j, s, HD : 2 * HD, :]) * scaled
            if s == 1:
                ovk[j, s, :HD, :] = output
                ovk[j, s, HD : 2 * HD, :] = grad_query
            else:
                oq_out[j, s // 2, :HD, :] = output.astype(bf16)
                oq_out[j, s // 2, HD:, :] = grad_query.astype(bf16)
            flipped = qd[j, rows(s), :].astype(f32).T
            ecols = pl.ds(s * 2 * tok, tok)
            fcols = pl.ds((s * 2 + 1) * tok, tok)
            wt[:HD, ecols] = (flipped[:HD] * share).astype(bf16)
            wt[HD:, ecols] = (flipped[HD:] * (-scaled * delta)).astype(bf16)
            wt[:HD, fcols] = jnp.zeros((HD, tok), bf16)
            wt[HD:, fcols] = (flipped[HD:] * scaled).astype(bf16)
        if last:
            send(OQ_HI, j)
            send(OQ_LO, j)
        else:
            pl.when(j == heads - 2)(functools.partial(combine, heads - 1))
        for kt in (3, 5, 0, 2, 4, 1):
            part = mm(ef[ring, rows(kt), :], wt[...], NT)
            if kt < 3:
                dkv_own[j, kt] = part
            else:
                dkv_out[j, kt - 3] = part.astype(bf16)
                send((DKV, DKV1, DKV2)[kt - 3], j)
            if last and kt == 2:
                hand_back(heads - 1)

    def hand_back(j):
        arrive(DKV, j)
        arrive(DKV2, j)
        for d, kind in ((0, DZ_HI), (2, DZ_LO)):
            dz_out[j, d // 2] = (dkv_own[j, d] + dkv_in[j, d].astype(f32)).astype(bf16)
            send(kind, j)

    def finish(j):
        for kind in (OQ_LO, OQ_HI, DKV1, DZ_LO, DZ_HI):
            arrive(kind, j)
        both = ovk[j, 1, : 2 * HD, :] + oq_in[j, 0].astype(f32) + oq_in[j, 1].astype(f32)
        both = both.T
        result[j, 0] = both[:, :HD].astype(bf16)
        result[j, 1] = both[:, HD:].astype(bf16)
        both = dkv_own[j, 1] + dkv_in[j, 1].astype(f32)
        both = both + dz_in[j, 0].astype(f32) + dz_in[j, 1].astype(f32)
        result[j, 2] = both[:, HD:].astype(bf16)
        result[j, 3] = both[:, :HD].astype(bf16)
        for n in range(4):
            output(j, n).start()

    def output(j, n):
        cols = pl.ds(pl.multiple_of(j * HD, HD), HD)
        target = (att_ref, gq_ref, gk_ref, gv_ref)[n].at[:, cols]
        return pltpu.make_async_copy(result.at[j, n], target, out_sem.at[j, n])

    def step(i, _):
        def first():
            send(ST_HI, i)
            pl.when(i + 1 < heads)(functools.partial(relay, i + 1))
            pl.when(i + AHEAD < heads)(functools.partial(send_own, 1, i + AHEAD))
            pl.when(i >= 2)(functools.partial(hand_back, i - 2))

        forward(i, (first, functools.partial(send, ST_LO, i), lambda: None))
        pl.when(i >= 3)(functools.partial(finish, i - 3))
        if heads == 1:
            combine(i)
        pl.when(i >= 1)(functools.partial(backward, False, i - 1))
        pl.when(i < heads - 1)(functools.partial(combine, i))
        pl.when(i + AHEAD < heads)(functools.partial(send_own, 0, i + AHEAD))

        @pl.when(i >= 1)
        def _():
            send(OQ_HI, i - 1)
            send(OQ_LO, i - 1)

        return 0

    lax.fori_loop(0, heads, step, 0)
    if heads > 1:
        hand_back(heads - 2)
    backward(True, heads - 1)
    for j in range(max(heads - 3, 0), heads - 1):
        finish(j)

    def drain(j, _):
        for kind in range(KINDS):
            sent_off(kind, j)
        return 0

    lax.fori_loop(0, heads, drain, 0)
    finish(heads - 1)

    def written(j, _):
        for n in range(4):
            output(j, n).wait()
        return 0

    lax.fori_loop(0, heads, written, 0)


def put(*refs):
    sources, targets, (held, take_sem, give_sem) = refs[:4], refs[4:8], refs[8:]
    takes = [pltpu.make_async_copy(sources[n], held.at[n], take_sem.at[n]) for n in range(4)]
    gives = [pltpu.make_async_copy(held.at[n], targets[n], give_sem.at[n]) for n in range(4)]
    for take in takes:
        take.start()
    for take, give in zip(takes, gives):
        take.wait()
        give.start()
    for give in gives:
        give.wait()


def on_device(queries, keys, values, reward_grad, window_mask):
    tok, width = queries.shape
    heads = width // HD
    frames = lax.axis_size("tile") // (GH * GW)
    bf16, f32 = jnp.bfloat16, jnp.float32
    hbm = pl.BlockSpec(memory_space=pltpu.MemorySpace.HBM)
    results = pl.pallas_call(
        functools.partial(kernel, heads, tok, frames),
        out_shape=[jax.ShapeDtypeStruct((tok, width), bf16)] * 4,
        in_specs=[pl.BlockSpec(memory_space=pltpu.SMEM), hbm, hbm, hbm, hbm],
        out_specs=[hbm] * 4,
        scratch_shapes=[
            pltpu.VMEM((heads, 3 * tok, 2 * HD), bf16),
            pltpu.VMEM((heads, 6 * tok, 2 * HD), bf16),
            pltpu.VMEM((ESUM, 6 * tok), bf16),
            [pltpu.VMEM((6 * tok, tok), f32)] * 2,
            [pltpu.VMEM((6 * tok, tok), f32)] * 2,
            pltpu.VMEM((8, tok), f32),
            pltpu.VMEM((2, 6 * tok, 6 * tok), bf16),
            pltpu.VMEM((heads, 3, 2 * ESUM - HD, tok), f32),
            pltpu.VMEM((2 * HD, 6 * tok), bf16),
            pltpu.VMEM((heads, 3, 8, tok), f32),
            pltpu.VMEM((heads, 2, 8, tok), f32),
            pltpu.VMEM((heads, 3, 8, tok), f32),
            pltpu.VMEM((heads, 2, 2 * HD, tok), bf16),
            pltpu.VMEM((heads, 2, 2 * HD, tok), bf16),
            pltpu.VMEM((heads, 3, tok, 2 * HD), f32),
            pltpu.VMEM((heads, 3, tok, 2 * HD), bf16),
            pltpu.VMEM((heads, 3, tok, 2 * HD), bf16),
            pltpu.VMEM((heads, 2, tok, 2 * HD), bf16),
            pltpu.VMEM((heads, 2, tok, 2 * HD), bf16),
            pltpu.VMEM((heads, 4, tok, HD), bf16),
            pltpu.SemaphoreType.DMA((2, heads)),
            pltpu.SemaphoreType.DMA((heads, 4)),
            pltpu.SemaphoreType.DMA((KINDS, heads)),
            pltpu.SemaphoreType.DMA((KINDS, heads)),
        ],
        compiler_params=pltpu.CompilerParams(
            collective_id=0, has_side_effects=True, vmem_limit_bytes=60 * 1024 * 1024
        ),
    )(window_mask, queries, keys, values, reward_grad)
    return pl.pallas_call(
        put,
        out_shape=[jax.ShapeDtypeStruct((tok, width), bf16)] * 4,
        in_specs=[hbm] * 4,
        out_specs=[hbm] * 4,
        scratch_shapes=[
            pltpu.VMEM((4, tok, width), bf16),
            pltpu.SemaphoreType.DMA((4,)),
            pltpu.SemaphoreType.DMA((4,)),
        ],
    )(*results)


def solution(mesh):
    return jax.shard_map(
        on_device,
        mesh=mesh,
        in_specs=(P("tile", "head"), P("tile", "head"), P("tile", "head"), P("tile", "head"), P()),
        out_specs=(P("tile", "head"), P("tile", "head"), P("tile", "head"), P("tile", "head")),
        check_vma=False,
    )
```
